32 devices in a mesh: grp: 2 (over x), pix: 16 (over z, y, core).
Axes of the slice: x: 2, y: 2, z: 4, core: 2. Of those that a mesh axis runs over, the one named last changes fastest.
Arguments:
- particle_images: bfloat16 [8192, 128, 128], P(('grp', 'pix')), parts along dimension 0, may hold values from -6 to 6
- defocus_group: int32 [8192], P(('grp', 'pix')), parts along dimension 0, may hold values from 0 to 63
- live_counts: int32 [32], P(('grp', 'pix')), parts along dimension 0, may hold values from 192 to 256, as said below
- defocus_values: float32 [128], P('grp'), parts along dimension 0, may hold values from 50 to 400
- test_matrix: bfloat16 [32768, 128], P(('grp', 'pix')), parts along dimension 0, may hold values from -0.046875 to 0.046875
Outputs:
- range_basis: bfloat16 [8192, 128], P(('grp', 'pix')), parts along dimension 0
- projection: float32 [32768, 128], P(('grp', 'pix')), parts along dimension 0
The draws below stay inside these ranges and needn't reach their ends.
There are 2 independent parts, one for each index of `grp`. The reference program is written for one: setup_inputs(seed, part) draws one part's arguments, and reference() takes and returns one part's arrays. A program takes and returns all parts, laid end to end along the dimension named above; each array names one. Nothing has to cross between parts.
Inputs may be any that keep to these rules, and one draw needn't show every extreme that they name: `live_counts`: each entry is the number of live particle slots of a shard, counted from its first slot; some shard is full in every draw.
All inputs are finite; a program needn't handle non-finite values.
Results may differ from the reference program's by a relative error of at most 0.011.
Values may be sent and summed in bfloat16 or wider, within the bound.
A program may use at most 192 MiB of HBM per device.

```python
import math
import jax
import jax.numpy as jnp
from jax import lax

SIDE = 128
RANK = 128
GROUPS = 64
PART_DEV = 256
PIX = 16384
SHARDS = 16
PARTICLES = 4096


def draw_live_counts(key, part):
    first_key, second_key = jax.random.split(jax.random.fold_in(key, 17))
    counts_all = jax.random.randint(first_key, (SHARDS,), 3 * PART_DEV // 4, PART_DEV + 1)
    full_shard = jax.random.randint(second_key, (), 0, SHARDS)
    return jnp.where(jnp.arange(SHARDS) == full_shard, PART_DEV, counts_all).astype(jnp.int32)


def with_ends(entries, own_key, smallest, high):
    shape = entries.shape
    place = [jax.random.randint(jax.random.fold_in(own_key, axis), (), 0, shape[axis]) for axis in range(len(shape))]
    entries = entries.at[tuple(place)].set(smallest)
    longest = shape.index(max(shape))
    place[longest] = (place[longest] + 1) % shape[longest]
    return entries.at[tuple(place)].set(high)


def shard_levels(rng, dims, cuts, least, top_value):
    level, own = 1.0, jax.random.fold_in(rng, 6)
    for dim, parts in cuts:
        steps = jnp.exp(jax.random.uniform(jax.random.fold_in(own, dim), (parts,), jnp.float32, least / len(cuts), top_value / len(cuts)))
        level = level * jnp.repeat(steps, dims[dim] // parts).reshape([-1 if axis == dim else 1 for axis in range(len(dims))])
    return level


def bell_draw(rng, dims, width, bound, cuts=(), kind=jnp.bfloat16):
    level = shard_levels(rng, dims, cuts, -0.22, 0.18) if cuts else 1.0
    drawn = jax.random.normal(rng, dims, jnp.float32) * width * level
    return jnp.minimum(jnp.maximum(drawn, -bound), bound).astype(kind)


def setup_inputs(seed: int = 0, part: int = 0) -> dict:
    splits = jax.random.split(jax.random.key(seed), 6)
    own_keys = jax.random.split(jax.random.fold_in(splits[5], part), 6)
    return {
        "particle_images": bell_draw(own_keys[0], (PARTICLES, SIDE, SIDE), 1.0, 6.0, ((0, 16),)),
        "defocus_group": with_ends(jax.random.randint(own_keys[1], (PARTICLES,), 0, GROUPS), jax.random.fold_in(own_keys[1], 1), 0, GROUPS - 1).astype(jnp.int32),
        "live_counts": draw_live_counts(jax.random.fold_in(jax.random.fold_in(splits[5], part), 71), part),
        "defocus_values": jnp.clip(jnp.exp(jax.random.uniform(own_keys[3], (GROUPS,), jnp.float32, math.log(50.0), math.log(400.0))), 50.0, 400.0),
        "test_matrix": bell_draw(own_keys[4], (PIX, RANK), PIX ** -0.5, 0.046875, ((0, 16),)),
    }


AMPLITUDE = 0.1
WIENER = 0.1

def frequency_sq(length):
    indices = jnp.arange(length, dtype=jnp.int32)
    frequency = jnp.where(indices < length // 2, indices, indices - length).astype(jnp.float32) / length
    return frequency[:, None] ** 2 + frequency[None, :] ** 2

def wiener_table(defocus_values, length):
    phases = jnp.pi * defocus_values[:, None, None] * frequency_sq(length)[None]
    contrast = -(math.sqrt(1.0 - AMPLITUDE ** 2) * jnp.sin(phases) + AMPLITUDE * jnp.cos(phases))
    return contrast / (contrast * contrast + WIENER)

def dft_tables(length):
    indices = jnp.arange(length, dtype=jnp.int32)
    product = indices[:, None] * indices[None, :] % length
    angles = 2.0 * math.pi / length * product.astype(jnp.float32)
    return (jnp.cos(angles).astype(jnp.bfloat16), jnp.sin(angles).astype(jnp.bfloat16))

def round_keep(values):
    return lax.optimization_barrier(values.astype(jnp.bfloat16)).astype(jnp.float32)

def left_mul(table_now, values_now):
    return jnp.einsum('uj,bjv->buv', table_now, values_now, precision=lax.Precision.HIGHEST)

def right_mul(values_now, table_now):
    return jnp.einsum('bjk,kv->bjv', values_now, table_now, precision=lax.Precision.HIGHEST)

def reference(particle_images, defocus_group, live_counts, defocus_values, test_matrix):
    filter_table = wiener_table(defocus_values, SIDE).astype(jnp.bfloat16).astype(jnp.float32)
    cos_b, sin_b = dft_tables(SIDE)
    cosine = cos_b.astype(jnp.float32)
    sine = sin_b.astype(jnp.float32)
    both_tables = jnp.concatenate([cosine, sine], axis=1)

    def correct(block_index):
        start_row = block_index * PART_DEV
        images_blk = lax.dynamic_slice_in_dim(particle_images, start_row, PART_DEV, 0).astype(jnp.float32)
        group_ids = lax.dynamic_slice_in_dim(defocus_group, start_row, PART_DEV, 0)
        filter_now = filter_table[group_ids]
        first_pass = round_keep(right_mul(images_blk, both_tables))
        cos_side = left_mul(cosine, first_pass)
        sin_side = left_mul(sine, first_pass)
        filt_re = round_keep((cos_side[..., :SIDE] - sin_side[..., SIDE:]) * filter_now)
        filt_im = round_keep(-(cos_side[..., SIDE:] + sin_side[..., :SIDE]) * filter_now)
        re_both = right_mul(filt_re, both_tables)
        im_both = right_mul(filt_im, both_tables)
        back_re = round_keep(re_both[..., :SIDE] - im_both[..., SIDE:])
        back_im = round_keep(re_both[..., SIDE:] + im_both[..., :SIDE])
        values = (left_mul(cosine, back_re) - left_mul(sine, back_im)) / float(SIDE * SIDE)
        live_rows = jnp.arange(PART_DEV, dtype=jnp.int32) < live_counts[block_index]
        values = jnp.where(live_rows[:, None, None], values, 0.0)
        return values.reshape(PART_DEV, PIX).astype(jnp.bfloat16)
    corrected = lax.map(correct, jnp.arange(SHARDS, dtype=jnp.int32)).reshape(PARTICLES, PIX)
    sketch = jnp.dot(corrected.astype(jnp.float32), test_matrix.astype(jnp.float32), preferred_element_type=jnp.float32)
    gram_matrix = jnp.dot(sketch.T, sketch, precision=lax.Precision.HIGHEST)
    factor_low = jnp.linalg.cholesky(gram_matrix)
    range_basis = lax.linalg.triangular_solve(factor_low, sketch, left_side=False, lower=True, transpose_a=True).astype(jnp.bfloat16)
    projection = jnp.dot(corrected.T.astype(jnp.float32), range_basis.astype(jnp.float32), preferred_element_type=jnp.float32)
    return (range_basis, projection)
```

```python
import functools
import math

import jax
import jax.numpy as jnp
from jax import lax
from jax.experimental import pallas as pl
from jax.experimental.pallas import tpu as pltpu
from jax.sharding import PartitionSpec as P

AMPLITUDE = 0.1
WIENER = 0.1
F32 = jnp.float32
BF16 = jnp.bfloat16
HIGHEST = lax.Precision.HIGHEST


def real_tables(length):
    rows = jnp.arange(length, dtype=jnp.int32)
    product = rows[:, None] * rows[None, :] % length
    angles = 2.0 * math.pi / length * product.astype(F32)
    packed = jnp.where(rows[None, :] <= length // 2, jnp.cos(angles), jnp.sin(angles))
    return packed.astype(BF16)


def phase_tables(defocus_values, length):
    index = jnp.arange(length, dtype=jnp.int32)
    freq = jnp.where(index < length // 2, index, index - length).astype(F32) / length
    phase = jnp.pi * defocus_values[:, None] * (freq * freq)[None, :]
    sine, cosine = jnp.sin(phase), jnp.cos(phase)
    keep = math.sqrt(1.0 - AMPLITUDE**2)
    first = -(keep * sine + AMPLITUDE * cosine)
    second = -(keep * cosine - AMPLITUDE * sine)
    return cosine, sine, first, second


def correct_kernel(
    group_ref,
    live_ref,
    image_ref,
    row_cos_ref,
    row_sin_ref,
    first_ref,
    second_ref,
    pair_ref,
    pair_t_ref,
    table_ref,
    table_t_ref,
    weight_ref,
    out_ref,
    filters,
    turned,
):
    step = pl.program_id(0)
    count, length, _ = image_ref.shape
    groups = filters.shape[0]

    @pl.when(step == 0)
    def _():
        def fill(group, carry):
            contrast = (
                first_ref[group] * row_cos_ref[pl.ds(group, 1), :]
                + second_ref[group] * row_sin_ref[pl.ds(group, 1), :]
            )
            wiener = contrast / (contrast * contrast + WIENER)
            filters[group] = wiener.astype(BF16).astype(F32) * weight_ref[...]
            return carry

        lax.fori_loop(0, groups, fill, 0)

    for pair in range(count // 2):
        images = jnp.concatenate([image_ref[2 * pair], image_ref[2 * pair + 1]], axis=1)
        weights = jnp.concatenate(
            [
                filters[group_ref[step * count + 2 * pair]],
                filters[group_ref[step * count + 2 * pair + 1]],
            ],
            axis=1,
        )
        rows = jnp.dot(images, pair_ref[...], preferred_element_type=F32).astype(BF16)
        spectrum = jnp.dot(table_t_ref[...], rows, preferred_element_type=F32)
        kept = (spectrum * weights).astype(BF16)
        back = jnp.dot(kept, pair_t_ref[...], preferred_element_type=F32).astype(BF16)
        result = jnp.dot(table_ref[...], back, preferred_element_type=F32)
        for half in range(2):
            turned[pl.ds(2 * pair + half, length, stride=count), :] = result[
                :, half * length : (half + 1) * length
            ]
    slot = step * count + lax.broadcasted_iota(jnp.int32, (1, count, 1), 1)
    values = turned[...].reshape(length, count, length)
    out_ref[...] = jnp.where(slot < live_ref[0], values, 0.0).astype(BF16)


def correct(images, groups, live, defocus_values):
    slots, length, _ = images.shape
    count = math.gcd(slots, 16)
    table = real_tables(length)
    zero = jnp.zeros_like(table)
    pair = jnp.concatenate(
        [jnp.concatenate([table, zero], axis=1), jnp.concatenate([zero, table], axis=1)], axis=0
    )
    cosine, sine, first, second = phase_tables(defocus_values, length)
    index = jnp.arange(length, dtype=jnp.int32)
    twice = jnp.where((index == 0) | (index == length // 2), 1.0, 2.0).astype(F32)
    weight = twice[:, None] * twice[None, :] / float(length * length)
    number = defocus_values.shape[0]

    def whole(*shape):
        return pl.BlockSpec(shape, lambda i, *_: (0,) * len(shape))

    return pl.pallas_call(
        correct_kernel,
        out_shape=jax.ShapeDtypeStruct((length, slots, length), BF16),
        grid_spec=pltpu.PrefetchScalarGridSpec(
            num_scalar_prefetch=2,
            grid=(slots // count,),
            in_specs=[
                pl.BlockSpec((count, length, length), lambda i, *_: (i, 0, 0)),
                whole(number, length),
                whole(number, length),
                whole(number, length, 1),
                whole(number, length, 1),
                whole(2 * length, 2 * length),
                whole(2 * length, 2 * length),
                whole(length, length),
                whole(length, length),
                whole(length, length),
            ],
            out_specs=pl.BlockSpec((length, count, length), lambda i, *_: (0, i, 0)),
            scratch_shapes=[
                pltpu.VMEM((number, length, length), F32),
                pltpu.VMEM((length * count, length), F32),
            ],
        ),
        compiler_params=pltpu.CompilerParams(vmem_limit_bytes=48 << 20),
        cost_estimate=pl.CostEstimate(
            flops=16 * slots * length**3, bytes_accessed=4 * slots * length**2, transcendentals=0
        ),
        name="correct",
    )(
        groups,
        live,
        images,
        cosine,
        sine,
        first[:, :, None],
        second[:, :, None],
        pair,
        pair.T,
        table,
        table.T,
        weight,
    )


def sketch_kernel(column_ref, matrix_ref, sketch_ref):
    @pl.when(pl.program_id(0) == 0)
    def _():
        sketch_ref[...] = jnp.zeros_like(sketch_ref)

    count, _, length = column_ref.shape
    total = sketch_ref[...]
    for pair in range(count // 2):
        left = jnp.concatenate([column_ref[2 * pair], column_ref[2 * pair + 1]], axis=1)
        right = matrix_ref[pl.ds(2 * pair * length, 2 * length), :]
        total += jnp.dot(left, right, preferred_element_type=F32)
    sketch_ref[...] = total


def make_sketch(columns, matrix):
    length, slots, _ = columns.shape
    rank = matrix.shape[1]
    count = math.gcd(length, 16)
    return pl.pallas_call(
        sketch_kernel,
        out_shape=jax.ShapeDtypeStruct((slots, rank), F32),
        grid=(length // count,),
        in_specs=[
            pl.BlockSpec((count, slots, length), lambda i: (i, 0, 0)),
            pl.BlockSpec((count * length, rank), lambda i: (i, 0)),
        ],
        out_specs=pl.BlockSpec((slots, rank), lambda i: (0, 0)),
        compiler_params=pltpu.CompilerParams(vmem_limit_bytes=48 << 20),
        name="sketch",
    )(columns, matrix)


def project_kernel(column_ref, sketch_ref, out_ref, halves):
    rank = sketch_ref.shape[1]

    @pl.when(pl.program_id(0) == 0)
    def _():
        high = sketch_ref[...].astype(BF16)
        halves[:, :rank] = high
        halves[:, rank:] = (sketch_ref[...] - high.astype(F32)).astype(BF16)

    count, _, length = column_ref.shape
    for row in range(count):
        both = lax.dot_general(
            column_ref[row], halves[...], (((0,), (0,)), ((), ())), preferred_element_type=F32
        )
        out_ref[pl.ds(row * length, length), :] = both[:, :rank] + both[:, rank:]


def project(columns, sketch):
    length, slots, _ = columns.shape
    rank = sketch.shape[1]
    count = math.gcd(length, 8)
    return pl.pallas_call(
        project_kernel,
        out_shape=jax.ShapeDtypeStruct((length * length, rank), F32),
        grid=(length // count,),
        in_specs=[
            pl.BlockSpec((count, slots, length), lambda i: (i, 0, 0)),
            pl.BlockSpec((slots, rank), lambda i: (0, 0)),
        ],
        out_specs=pl.BlockSpec((count * length, rank), lambda i: (i, 0)),
        scratch_shapes=[pltpu.VMEM((slots, 2 * rank), BF16)],
        compiler_params=pltpu.CompilerParams(vmem_limit_bytes=48 << 20),
        name="project",
    )(columns, sketch)


def per_device(particle_images, defocus_group, live_counts, defocus_values, test_matrix):
    matrix = lax.all_gather(test_matrix, "pix", axis=0, tiled=True)
    columns = correct(particle_images, defocus_group, live_counts, defocus_values)
    sketch = make_sketch(columns, matrix)
    gram = lax.psum(jnp.dot(sketch.T, sketch, precision=HIGHEST), "pix")
    summed = lax.psum_scatter(project(columns, sketch), "pix", scatter_dimension=0, tiled=True)
    factor_low = jnp.linalg.cholesky(gram)
    rank = gram.shape[0]
    inverse_t = lax.linalg.triangular_solve(
        factor_low, jnp.eye(rank, dtype=F32), left_side=False, lower=True, transpose_a=True
    )
    range_basis = jnp.dot(sketch, inverse_t, precision=HIGHEST).astype(BF16)
    projection = jnp.dot(summed, inverse_t, precision=HIGHEST)
    return (range_basis, projection)


def solution(mesh):
    placed = (
        P(("grp", "pix"), None, None),
        P(("grp", "pix")),
        P(("grp", "pix")),
        P("grp"),
        P(("grp", "pix"), None),
    )
    return jax.shard_map(
        per_device,
        mesh=mesh,
        in_specs=placed,
        out_specs=(P(("grp", "pix"), None), P(("grp", "pix"), None)),
        check_vma=False,
    )
```

```python
import functools
import math

import jax
import jax.numpy as jnp
from jax import lax
from jax.experimental import pallas as pl
from jax.experimental.pallas import tpu as pltpu
from jax.sharding import PartitionSpec as P

AMPLITUDE = 0.1
WIENER = 0.1
F32 = jnp.float32
BF16 = jnp.bfloat16
HIGHEST = lax.Precision.HIGHEST


def real_tables(length):
    rows = jnp.arange(length, dtype=jnp.int32)
    product = rows[:, None] * rows[None, :] % length
    angles = 2.0 * math.pi / length * product.astype(F32)
    packed = jnp.where(rows[None, :] <= length // 2, jnp.cos(angles), jnp.sin(angles))
    return packed.astype(BF16)


def filter_table(defocus_values, length):
    index = jnp.arange(length, dtype=jnp.int32)
    freq = jnp.where(index < length // 2, index, index - length).astype(F32) / length
    phase = jnp.pi * defocus_values[:, None] * (freq * freq)[None, :]
    sine, cosine = lax.optimization_barrier((jnp.sin(phase), jnp.cos(phase)))
    keep = math.sqrt(1.0 - AMPLITUDE**2)
    first = (keep * sine + AMPLITUDE * cosine)[:, :, None]
    second = (keep * cosine - AMPLITUDE * sine)[:, :, None]
    contrast = -(first * cosine[:, None, :] + second * sine[:, None, :])
    wiener = (contrast / (contrast * contrast + WIENER)).astype(BF16).astype(F32)
    twice = jnp.where((index == 0) | (index == length // 2), 1.0, 2.0).astype(F32)
    return (wiener * (twice[:, None] * twice[None, :] / float(length * length))).astype(BF16)


def correct_kernel(
    group_ref,
    live_ref,
    image_ref,
    filters,
    pair_ref,
    pair_t_ref,
    table_ref,
    table_t_ref,
    out_ref,
    turned,
):
    step = pl.program_id(0)
    count, length, _ = image_ref.shape
    pairs = count // 2
    base = step * count

    def side_by_side(parts):
        return jnp.concatenate(parts, axis=1)

    def stacked(wide):
        return jnp.concatenate(
            [wide[:, 2 * length * i : 2 * length * (i + 1)] for i in range(pairs)], axis=0
        )

    def unstacked(tall):
        return side_by_side([tall[length * i : length * (i + 1)] for i in range(pairs)])

    images = jnp.concatenate(
        [side_by_side([image_ref[2 * i], image_ref[2 * i + 1]]) for i in range(pairs)], axis=0
    )
    rows = jnp.dot(images, pair_ref[...], preferred_element_type=F32).astype(BF16)
    spectrum = jnp.dot(table_t_ref[...], unstacked(rows), preferred_element_type=F32)
    weights = side_by_side([filters[group_ref[base + i]] for i in range(count)])
    kept = (spectrum * weights.astype(F32)).astype(BF16)
    back = jnp.dot(stacked(kept), pair_t_ref[...], preferred_element_type=F32).astype(BF16)
    result = jnp.dot(table_ref[...], unstacked(back), preferred_element_type=F32)
    for i in range(count):
        turned[pl.ds(i, length, stride=count), :] = result[:, i * length : (i + 1) * length]
    slot = base + lax.broadcasted_iota(jnp.int32, (1, count, 1), 1)
    values = turned[...].reshape(length, count, length)
    out_ref[...] = jnp.where(slot < live_ref[0], values, 0.0).astype(BF16)


def correct(images, groups, live, defocus_values):
    slots, length, _ = images.shape
    count = math.gcd(slots, 16)
    table = real_tables(length)
    zero = jnp.zeros_like(table)
    pair = jnp.concatenate(
        [jnp.concatenate([table, zero], axis=1), jnp.concatenate([zero, table], axis=1)], axis=0
    )
    number = defocus_values.shape[0]

    def whole(*shape):
        return pl.BlockSpec(shape, lambda i, *_: (0,) * len(shape))

    return pl.pallas_call(
        correct_kernel,
        out_shape=jax.ShapeDtypeStruct((length, slots, length), BF16),
        grid_spec=pltpu.PrefetchScalarGridSpec(
            num_scalar_prefetch=2,
            grid=(slots // count,),
            in_specs=[
                pl.BlockSpec((count, length, length), lambda i, *_: (i, 0, 0)),
                whole(number, length, length),
                whole(2 * length, 2 * length),
                whole(2 * length, 2 * length),
                whole(length, length),
                whole(length, length),
            ],
            out_specs=pl.BlockSpec((length, count, length), lambda i, *_: (0, i, 0)),
            scratch_shapes=[pltpu.VMEM((length * count, length), F32)],
        ),
        compiler_params=pltpu.CompilerParams(vmem_limit_bytes=48 << 20),
        cost_estimate=pl.CostEstimate(
            flops=16 * slots * length**3, bytes_accessed=4 * slots * length**2, transcendentals=0
        ),
        name="correct",
    )(groups, live, images, filter_table(defocus_values, length), pair, pair.T, table, table.T)


def sketch_kernel(column_ref, matrix_ref, sketch_ref):
    @pl.when(pl.program_id(0) == 0)
    def _():
        sketch_ref[...] = jnp.zeros_like(sketch_ref)

    count, _, length = column_ref.shape
    total = sketch_ref[...]
    for pair in range(count // 2):
        left = jnp.concatenate([column_ref[2 * pair], column_ref[2 * pair + 1]], axis=1)
        right = matrix_ref[pl.ds(2 * pair * length, 2 * length), :]
        total += jnp.dot(left, right, preferred_element_type=F32)
    sketch_ref[...] = total


def make_sketch(columns, matrix):
    length, slots, _ = columns.shape
    rank = matrix.shape[1]
    count = math.gcd(length, 16)
    return pl.pallas_call(
        sketch_kernel,
        out_shape=jax.ShapeDtypeStruct((slots, rank), F32),
        grid=(length // count,),
        in_specs=[
            pl.BlockSpec((count, slots, length), lambda i: (i, 0, 0)),
            pl.BlockSpec((count * length, rank), lambda i: (i, 0)),
        ],
        out_specs=pl.BlockSpec((slots, rank), lambda i: (0, 0)),
        compiler_params=pltpu.CompilerParams(vmem_limit_bytes=48 << 20),
        name="sketch",
    )(columns, matrix)


def bits_of(size):
    return size.bit_length() - 1


def partner_of(me, mask):
    for shift in range(mask.bit_length()):
        bit = 1 << shift
        if mask & bit:
            me = me + bit * (1 - 2 * lax.rem(lax.div(me, bit), 2))
    return me


def greet(me, size):
    barrier = pltpu.get_barrier_semaphore()
    for shift in range(bits_of(size)):
        pl.semaphore_signal(
            barrier,
            inc=1,
            device_id={"pix": partner_of(me, 1 << shift)},
            device_id_type=pl.DeviceIdType.MESH,
        )
    pl.semaphore_wait(barrier, bits_of(size))


def sum_kernel(size, part_ref, out_ref, arrived, send_sem, recv_sem):
    me = lax.axis_index("pix")
    greet(me, size)
    out_ref[...] = part_ref[...]
    for stage in range(bits_of(size)):
        copy = pltpu.make_async_remote_copy(
            src_ref=out_ref,
            dst_ref=arrived.at[stage],
            send_sem=send_sem.at[stage],
            recv_sem=recv_sem.at[stage],
            device_id={"pix": partner_of(me, 1 << stage)},
            device_id_type=pl.DeviceIdType.MESH,
        )
        copy.start()
        copy.wait()
        out_ref[...] += arrived[stage]


def sum_over_shards(part, size):
    stages = bits_of(size)
    return pl.pallas_call(
        functools.partial(sum_kernel, size),
        out_shape=jax.ShapeDtypeStruct(part.shape, part.dtype),
        in_specs=[pl.BlockSpec(memory_space=pltpu.VMEM)],
        out_specs=pl.BlockSpec(memory_space=pltpu.VMEM),
        scratch_shapes=[
            pltpu.VMEM((stages,) + part.shape, part.dtype),
            pltpu.SemaphoreType.DMA((stages,)),
            pltpu.SemaphoreType.DMA((stages,)),
        ],
        compiler_params=pltpu.CompilerParams(collective_id=0, has_side_effects=True),
        name="sum_over_shards",
    )(part)


def halving_orders(size):
    bits = [1 << shift for shift in range(bits_of(size))]
    if len(bits) < 3:
        return (bits, bits)
    return (bits, bits[:1] + bits[2:] + bits[1:2])


def masks_of(bits):
    if not bits:
        return [0]
    rest = masks_of(bits[1:])
    return [bits[0] | mask for mask in rest] + rest


def project_kernel(size, basis_ref, column_ref, out_ref, held, arrived, send_sem, recv_sem):
    me = lax.axis_index("pix")
    length = column_ref.shape[0]
    rows = length // size
    part = rows // 2
    orders = halving_orders(size)
    slots = {}
    for half in range(2):
        for stage in range(len(orders[half])):
            for mask in masks_of(orders[half][stage + 1 :]):
                slots[half, stage, mask] = len(slots) % (size - 1)

    def copy_of(half, stage, mask):
        bit = orders[half][stage]
        slot = slots[half, stage, mask]
        return pltpu.make_async_remote_copy(
            src_ref=held.at[half, bit | mask],
            dst_ref=arrived.at[half, slot],
            send_sem=send_sem.at[half, slot],
            recv_sem=recv_sem.at[half, slot],
            device_id={"pix": partner_of(me, bit)},
            device_id_type=pl.DeviceIdType.MESH,
        )

    greet(me, size)
    first = orders[0][0]
    order = masks_of([first] + orders[0][1:])
    for mask in order:
        start = partner_of(me, mask) * rows
        for half in range(2):
            right = jnp.concatenate(
                [column_ref[start + half * part + row] for row in range(part)], axis=1
            )
            held[half, mask] = jnp.dot(
                basis_ref[...], right, preferred_element_type=F32
            ).astype(BF16)
            if mask & first:
                copy_of(half, 0, mask - first).start()

    for stage in range(bits_of(size)):
        for half in range(2):
            later = orders[half][stage + 1 :]
            for mask in masks_of(later):
                copy_of(half, stage, mask).wait_recv()
                total = (
                    held[half, mask].astype(F32)
                    + arrived[half, slots[half, stage, mask]].astype(F32)
                )
                if later:
                    held[half, mask] = total.astype(BF16)
                    if mask & later[0]:
                        copy_of(half, stage + 1, mask - later[0]).start()
                else:
                    turned = total.T
                    height = out_ref.shape[0] // 2
                    out_ref[half * height : (half + 1) * height, :] = turned
    for half in range(2):
        for stage in range(bits_of(size)):
            for mask in masks_of(orders[half][stage + 1 :]):
                copy_of(half, stage, mask).wait_send()


def project(columns, basis, size):
    length, slots, _ = columns.shape
    rank = basis.shape[1]
    width = length * length // size
    return pl.pallas_call(
        functools.partial(project_kernel, size),
        out_shape=jax.ShapeDtypeStruct((width, rank), F32),
        in_specs=[pl.BlockSpec(memory_space=pltpu.VMEM)] * 2,
        out_specs=pl.BlockSpec(memory_space=pltpu.VMEM),
        scratch_shapes=[
            pltpu.VMEM((2, size, rank, width // 2), BF16),
            pltpu.VMEM((2, size - 1, rank, width // 2), BF16),
            pltpu.SemaphoreType.DMA((2, size - 1)),
            pltpu.SemaphoreType.DMA((2, size - 1)),
        ],
        compiler_params=pltpu.CompilerParams(
            collective_id=1, has_side_effects=True, vmem_limit_bytes=48 << 20
        ),
        name="project",
    )(basis.T, columns)


def per_device(particle_images, defocus_group, live_counts, defocus_values, test_matrix):
    size = lax.axis_size("pix")
    matrix = lax.all_gather(test_matrix, "pix", axis=0, tiled=True)
    columns = correct(particle_images, defocus_group, live_counts, defocus_values)
    sketch = make_sketch(columns, matrix)
    gram = sum_over_shards(jnp.dot(sketch.T, sketch, precision=HIGHEST), size)
    factor_low = jnp.linalg.cholesky(gram)
    rank = gram.shape[0]
    inverse_t = lax.linalg.triangular_solve(
        factor_low, jnp.eye(rank, dtype=F32), left_side=False, lower=True, transpose_a=True
    )
    range_basis = jnp.dot(sketch, inverse_t, precision=HIGHEST).astype(BF16)
    return (range_basis, project(columns, range_basis, size))


def solution(mesh):
    placed = (
        P(("grp", "pix"), None, None),
        P(("grp", "pix")),
        P(("grp", "pix")),
        P("grp"),
        P(("grp", "pix"), None),
    )
    return jax.shard_map(
        per_device,
        mesh=mesh,
        in_specs=placed,
        out_specs=(P(("grp", "pix"), None), P(("grp", "pix"), None)),
        check_vma=False,
    )
```

```python
import functools
import math

import jax
import jax.numpy as jnp
from jax import lax
from jax.experimental import pallas as pl
from jax.experimental.pallas import tpu as pltpu
from jax.sharding import PartitionSpec as P

AMPLITUDE = 0.1
WIENER = 0.1
F32 = jnp.float32
BF16 = jnp.bfloat16
HIGHEST = lax.Precision.HIGHEST


def real_tables(length):
    rows = jnp.arange(length, dtype=jnp.int32)
    product = rows[:, None] * rows[None, :] % length
    angles = 2.0 * math.pi / length * product.astype(F32)
    packed = jnp.where(rows[None, :] <= length // 2, jnp.cos(angles), jnp.sin(angles))
    return packed.astype(BF16)


def filter_table(defocus_values, length):
    index = jnp.arange(length, dtype=jnp.int32)
    freq = jnp.where(index < length // 2, index, index - length).astype(F32) / length
    phase = jnp.pi * defocus_values[:, None] * (freq * freq)[None, :]
    sine, cosine = lax.optimization_barrier((jnp.sin(phase), jnp.cos(phase)))
    keep = math.sqrt(1.0 - AMPLITUDE**2)
    first = (keep * sine + AMPLITUDE * cosine)[:, :, None]
    second = (keep * cosine - AMPLITUDE * sine)[:, :, None]
    contrast = -(first * cosine[:, None, :] + second * sine[:, None, :])
    wiener = (contrast / (contrast * contrast + WIENER)).astype(BF16).astype(F32)
    twice = jnp.where((index == 0) | (index == length // 2), 1.0, 2.0).astype(F32)
    return (wiener * (twice[:, None] * twice[None, :] / float(length * length))).astype(BF16)


def bits_of(size):
    return size.bit_length() - 1


def partner_of(me, mask):
    for shift in range(mask.bit_length()):
        bit = 1 << shift
        if mask & bit:
            me = me + bit * (1 - 2 * lax.rem(lax.div(me, bit), 2))
    return me


def greet(me, masks):
    barrier = pltpu.get_barrier_semaphore()
    for mask in masks:
        pl.semaphore_signal(
            barrier,
            inc=1,
            device_id={"pix": partner_of(me, mask)},
            device_id_type=pl.DeviceIdType.MESH,
        )
    pl.semaphore_wait(barrier, len(masks))


def remote(src, dst, send_sem, recv_sem, peer):
    return pltpu.make_async_remote_copy(
        src_ref=src,
        dst_ref=dst,
        send_sem=send_sem,
        recv_sem=recv_sem,
        device_id={"pix": peer},
        device_id_type=pl.DeviceIdType.MESH,
    )


def halving_orders(size):
    bits = [1 << shift for shift in range(bits_of(size))]
    if len(bits) < 3:
        return (bits, bits)
    return (bits, bits[:1] + bits[2:] + bits[1:2])


def masks_of(bits):
    if not bits:
        return [0]
    rest = masks_of(bits[1:])
    return [bits[0] | mask for mask in rest] + rest


def gathering_orders(size):
    first, second = halving_orders(size)
    return (first[::-1], second[1:][::-1] + second[:1])


def sums(bits):
    out = [0]
    for bit in bits:
        out = out + [bit | mask for mask in out]
    return out


def direct_sum(rank, size):
    return rank % (8 * size) == 0


def peers(rank, size):
    if direct_sum(rank, size):
        return list(range(1, size))
    return [1 << shift for shift in range(bits_of(size))]


def sum_gram(me, size, gram_ref, parts, arrived, send_sem, recv_sem):
    if not direct_sum(parts.shape[0] * parts.shape[1], size):
        gram_ref[...] = parts[...].reshape(gram_ref.shape)
        for stage in range(bits_of(size)):
            copy = remote(
                gram_ref,
                arrived.at[stage],
                send_sem.at[stage],
                recv_sem.at[stage],
                partner_of(me, 1 << stage),
            )
            copy.start()
            copy.wait()
            gram_ref[...] += arrived[stage]
        return
    height = parts.shape[1]
    scatter = [
        remote(
            parts.at[partner_of(me, d)],
            arrived.at[d],
            send_sem.at[d],
            recv_sem.at[d],
            partner_of(me, d),
        )
        for d in range(1, size)
    ]
    for copy in scatter:
        copy.start()
    total = parts[me]
    for d, copy in enumerate(scatter, 1):
        copy.wait_recv()
        total = total + arrived[d]
    arrived[0] = total
    own = pl.ds(pl.multiple_of(me * height, height), height)
    gather = [
        remote(
            arrived.at[0],
            gram_ref.at[own],
            send_sem.at[size + d],
            recv_sem.at[size + d],
            partner_of(me, d),
        )
        for d in range(1, size)
    ]
    for copy in gather:
        copy.start()
    gram_ref[own, :] = total
    for copy in gather:
        copy.wait_recv()
    for copy in scatter + gather:
        copy.wait_send()


def sketch_kernel(
    size,
    group_ref,
    live_ref,
    image_ref,
    matrix_ref,
    filters,
    pair_ref,
    pair_t_ref,
    table_ref,
    table_t_ref,
    out_ref,
    sketch_ref,
    gram_ref,
    turned,
    held,
    summed,
    parts,
    arrived,
    send_sem,
    recv_sem,
    sum_send_sem,
    sum_recv_sem,
):
    me = lax.axis_index("pix")
    step = pl.program_id(0)
    steps = out_ref.shape[1] // image_ref.shape[0]
    count, length, _ = image_ref.shape
    pairs = count // 2
    base = step * count
    orders = gathering_orders(size)
    stages = bits_of(size)
    height = matrix_ref.shape[0] // 2

    def copy_of(half, stage, mask):
        bit = orders[half][stage]
        slot = (bit | mask) - 1
        return remote(
            held.at[half, mask],
            held.at[half, bit | mask],
            send_sem.at[half, slot],
            recv_sem.at[half, slot],
            partner_of(me, bit),
        )

    def receive(stage, half, mask):
        copy_of(half, stage, mask).wait_recv()
        for later in range(stage + 1, stages):
            copy_of(half, later, orders[half][stage] | mask).start()

    @pl.when(step == 0)
    def _():
        greet(me, peers(gram_ref.shape[0], size))
        for half in range(2):
            held[half, 0] = matrix_ref[half * height : (half + 1) * height, :]
        for stage in range(stages):
            for half in range(2):
                copy_of(half, stage, 0).start()

    early = min(2, stages)
    for stage in range(early):

        @pl.when(step == steps * (5 + 6 * stage) // 16)
        def _(stage=stage):
            for place in range(1 << stage):
                for half in range(2):
                    receive(stage, half, sums(orders[half][:stage])[place])

    def side_by_side(values):
        return jnp.concatenate(values, axis=1)

    def stacked(wide):
        return jnp.concatenate(
            [wide[:, 2 * length * i : 2 * length * (i + 1)] for i in range(pairs)], axis=0
        )

    def unstacked(tall):
        return side_by_side([tall[length * i : length * (i + 1)] for i in range(pairs)])

    images = jnp.concatenate(
        [side_by_side([image_ref[2 * i], image_ref[2 * i + 1]]) for i in range(pairs)], axis=0
    )
    rows = jnp.dot(images, pair_ref[...], preferred_element_type=F32).astype(BF16)
    spectrum = jnp.dot(table_t_ref[...], unstacked(rows), preferred_element_type=F32)
    weights = side_by_side([filters[group_ref[base + i]] for i in range(count)])
    kept = (spectrum * weights.astype(F32)).astype(BF16)
    back = jnp.dot(stacked(kept), pair_t_ref[...], preferred_element_type=F32).astype(BF16)
    result = jnp.dot(table_ref[...], unstacked(back), preferred_element_type=F32)
    for i in range(count):
        turned[pl.ds(i, length, stride=count), :] = result[:, i * length : (i + 1) * length]
    slot = base + lax.broadcasted_iota(jnp.int32, (1, count, 1), 1)
    values = turned[...].reshape(length, count, length)
    out_ref[:, pl.ds(pl.multiple_of(base, count), count), :] = jnp.where(
        slot < live_ref[0], values, 0.0
    ).astype(BF16)

    @pl.when(step == steps - 1)
    def _():
        lines = length // size
        part = lines // 2

        def term(half, mask):
            start = partner_of(me, mask) * lines + half * part
            left = side_by_side([out_ref[start + line] for line in range(part)])
            return jnp.dot(left, held[half, mask], preferred_element_type=F32)

        sketch_ref[...] = jnp.zeros_like(sketch_ref)
        for half in range(2):
            for mask in sums(orders[half][:early]):
                sketch_ref[...] += term(half, mask)
        for stage in range(early, stages):
            for place in range(1 << stage):
                for half in range(2):
                    mask = sums(orders[half][:stage])[place]
                    receive(stage, half, mask)
                    sketch_ref[...] += term(half, orders[half][stage] | mask)
        sketch = sketch_ref[...]
        gram = lax.dot_general(
            sketch, sketch, (((0,), (0,)), ((), ())), precision=HIGHEST, preferred_element_type=F32
        )
        parts[...] = gram.reshape(parts.shape)
        sum_gram(me, size, summed, parts, arrived, sum_send_sem, sum_recv_sem)
        gram_ref[...] = summed[...]
        for half in range(2):
            for stage in range(stages):
                for mask in sums(orders[half][:stage]):
                    copy_of(half, stage, mask).wait_send()


def make_sketch(images, groups, live, defocus_values, matrix, size):
    slots, length, _ = images.shape
    height, rank = matrix.shape
    count = math.gcd(slots, 16)
    table = real_tables(length)
    zero = jnp.zeros_like(table)
    pair = jnp.concatenate(
        [jnp.concatenate([table, zero], axis=1), jnp.concatenate([zero, table], axis=1)], axis=0
    )
    number = defocus_values.shape[0]
    if direct_sum(rank, size):
        summing = [
            pltpu.VMEM((size, rank // size, rank), F32),
            pltpu.VMEM((size, rank // size, rank), F32),
        ]
        signals = 2 * size
    else:
        summing = [
            pltpu.VMEM((1, rank, rank), F32),
            pltpu.VMEM((bits_of(size), rank, rank), F32),
        ]
        signals = bits_of(size)

    def whole(*shape):
        return pl.BlockSpec(shape, lambda i, *_: (0,) * len(shape))

    return pl.pallas_call(
        functools.partial(sketch_kernel, size),
        out_shape=(
            jax.ShapeDtypeStruct((length, slots, length), BF16),
            jax.ShapeDtypeStruct((slots, rank), F32),
            jax.ShapeDtypeStruct((rank, rank), F32),
        ),
        grid_spec=pltpu.PrefetchScalarGridSpec(
            num_scalar_prefetch=2,
            grid=(slots // count,),
            in_specs=[
                pl.BlockSpec((count, length, length), lambda i, *_: (i, 0, 0)),
                whole(height, rank),
                whole(number, length, length),
                whole(2 * length, 2 * length),
                whole(2 * length, 2 * length),
                whole(length, length),
                whole(length, length),
            ],
            out_specs=(whole(length, slots, length), whole(slots, rank), whole(rank, rank)),
            scratch_shapes=[
                pltpu.VMEM((length * count, length), F32),
                pltpu.VMEM((2, size, height // 2, rank), BF16),
                pltpu.VMEM((rank, rank), F32),
                *summing,
                pltpu.SemaphoreType.DMA((2, size - 1)),
                pltpu.SemaphoreType.DMA((2, size - 1)),
                pltpu.SemaphoreType.DMA((signals,)),
                pltpu.SemaphoreType.DMA((signals,)),
            ],
        ),
        compiler_params=pltpu.CompilerParams(
            collective_id=0, has_side_effects=True, vmem_limit_bytes=50 << 20
        ),
        name="sketch",
    )(
        groups,
        live,
        images,
        matrix,
        filter_table(defocus_values, length),
        pair,
        pair.T,
        table,
        table.T,
    )


def project_kernel(size, basis_ref, column_ref, out_ref, held, arrived, send_sem, recv_sem):
    me = lax.axis_index("pix")
    length = column_ref.shape[0]
    rows = length // size
    part = rows // 2
    orders = halving_orders(size)
    slots = {}
    for half in range(2):
        for stage in range(len(orders[half])):
            for mask in masks_of(orders[half][stage + 1 :]):
                slots[half, stage, mask] = len(slots) % (size - 1)

    def copy_of(half, stage, mask):
        bit = orders[half][stage]
        slot = slots[half, stage, mask]
        return remote(
            held.at[half, bit | mask],
            arrived.at[half, slot],
            send_sem.at[half, slot],
            recv_sem.at[half, slot],
            partner_of(me, bit),
        )

    greet(me, [1 << shift for shift in range(bits_of(size))])
    first = orders[0][0]
    order = masks_of([first] + orders[0][1:])
    for mask in order:
        start = partner_of(me, mask) * rows
        for half in range(2):
            right = jnp.concatenate(
                [column_ref[start + half * part + row] for row in range(part)], axis=1
            )
            held[half, mask] = jnp.dot(
                basis_ref[...], right, preferred_element_type=F32
            ).astype(BF16)
            if mask & first:
                copy_of(half, 0, mask - first).start()

    for stage in range(bits_of(size)):
        for half in range(2):
            later = orders[half][stage + 1 :]
            for mask in masks_of(later):
                copy_of(half, stage, mask).wait_recv()
                total = (
                    held[half, mask].astype(F32)
                    + arrived[half, slots[half, stage, mask]].astype(F32)
                )
                if later:
                    held[half, mask] = total.astype(BF16)
                    if mask & later[0]:
                        copy_of(half, stage + 1, mask - later[0]).start()
                else:
                    turned = total.T
                    height = out_ref.shape[0] // 2
                    out_ref[half * height : (half + 1) * height, :] = turned
    for half in range(2):
        for stage in range(bits_of(size)):
            for mask in masks_of(orders[half][stage + 1 :]):
                copy_of(half, stage, mask).wait_send()


def project(columns, basis, size):
    length, slots, _ = columns.shape
    rank = basis.shape[1]
    width = length * length // size
    return pl.pallas_call(
        functools.partial(project_kernel, size),
        out_shape=jax.ShapeDtypeStruct((width, rank), F32),
        in_specs=[pl.BlockSpec(memory_space=pltpu.VMEM)] * 2,
        out_specs=pl.BlockSpec(memory_space=pltpu.VMEM),
        scratch_shapes=[
            pltpu.VMEM((2, size, rank, width // 2), BF16),
            pltpu.VMEM((2, size - 1, rank, width // 2), BF16),
            pltpu.SemaphoreType.DMA((2, size - 1)),
            pltpu.SemaphoreType.DMA((2, size - 1)),
        ],
        compiler_params=pltpu.CompilerParams(
            collective_id=1, has_side_effects=True, vmem_limit_bytes=48 << 20
        ),
        name="project",
    )(basis.T, columns)


def per_device(particle_images, defocus_group, live_counts, defocus_values, test_matrix):
    size = lax.axis_size("pix")
    columns, sketch, gram = make_sketch(
        particle_images, defocus_group, live_counts, defocus_values, test_matrix, size
    )
    factor_low = jnp.linalg.cholesky(gram)
    rank = gram.shape[0]
    inverse_t = lax.linalg.triangular_solve(
        factor_low, jnp.eye(rank, dtype=F32), left_side=False, lower=True, transpose_a=True
    )
    range_basis = jnp.dot(sketch, inverse_t, precision=HIGHEST).astype(BF16)
    return (range_basis, project(columns, range_basis, size))


def solution(mesh):
    placed = (
        P(("grp", "pix"), None, None),
        P(("grp", "pix")),
        P(("grp", "pix")),
        P("grp"),
        P(("grp", "pix"), None),
    )
    return jax.shard_map(
        per_device,
        mesh=mesh,
        in_specs=placed,
        out_specs=(P(("grp", "pix"), None), P(("grp", "pix"), None)),
        check_vma=False,
    )
```

```python
import functools
import math

import jax
import jax.numpy as jnp
from jax import lax
from jax.experimental import pallas as pl
from jax.experimental.pallas import tpu as pltpu
from jax.sharding import PartitionSpec as P

AMPLITUDE = 0.1
WIENER = 0.1
F32 = jnp.float32
BF16 = jnp.bfloat16
HIGHEST = lax.Precision.HIGHEST


def real_tables(length):
    rows = jnp.arange(length, dtype=jnp.int32)
    product = rows[:, None] * rows[None, :] % length
    angles = 2.0 * math.pi / length * product.astype(F32)
    packed = jnp.where(rows[None, :] <= length // 2, jnp.cos(angles), jnp.sin(angles))
    return packed.astype(BF16)


def filter_table(defocus_values, length):
    index = jnp.arange(length, dtype=jnp.int32)
    freq = jnp.where(index < length // 2, index, index - length).astype(F32) / length
    phase = jnp.pi * defocus_values[:, None] * (freq * freq)[None, :]
    sine, cosine = lax.optimization_barrier((jnp.sin(phase), jnp.cos(phase)))
    keep = math.sqrt(1.0 - AMPLITUDE**2)
    first = (keep * sine + AMPLITUDE * cosine)[:, :, None]
    second = (keep * cosine - AMPLITUDE * sine)[:, :, None]
    contrast = -(first * cosine[:, None, :] + second * sine[:, None, :])
    wiener = (contrast / (contrast * contrast + WIENER)).astype(BF16).astype(F32)
    twice = jnp.where((index == 0) | (index == length // 2), 1.0, 2.0).astype(F32)
    return (wiener * (twice[:, None] * twice[None, :] / float(length * length))).astype(BF16)


def bits_of(size):
    return size.bit_length() - 1


def partner_of(me, mask):
    for shift in range(mask.bit_length()):
        bit = 1 << shift
        if mask & bit:
            me = me + bit * (1 - 2 * lax.rem(lax.div(me, bit), 2))
    return me


def greet(me, masks):
    barrier = pltpu.get_barrier_semaphore()
    for mask in masks:
        pl.semaphore_signal(
            barrier,
            inc=1,
            device_id={"pix": partner_of(me, mask)},
            device_id_type=pl.DeviceIdType.MESH,
        )
    pl.semaphore_wait(barrier, len(masks))


def remote(src, dst, send_sem, recv_sem, peer):
    return pltpu.make_async_remote_copy(
        src_ref=src,
        dst_ref=dst,
        send_sem=send_sem,
        recv_sem=recv_sem,
        device_id={"pix": peer},
        device_id_type=pl.DeviceIdType.MESH,
    )


def halving_orders(size):
    bits = [1 << shift for shift in range(bits_of(size))]
    if len(bits) < 3:
        return (bits, bits)
    return (bits, bits[:1] + bits[2:] + bits[1:2])


def masks_of(bits):
    if not bits:
        return [0]
    rest = masks_of(bits[1:])
    return [bits[0] | mask for mask in rest] + rest


def gathering_orders(size):
    first, second = halving_orders(size)
    return (first[::-1], second[1:][::-1] + second[:1])


def sums(bits):
    out = [0]
    for bit in bits:
        out = out + [bit | mask for mask in out]
    return out


def direct_sum(rank, size):
    return rank % (8 * size) == 0


def peers(rank, size):
    if direct_sum(rank, size):
        return list(range(1, size))
    return [1 << shift for shift in range(bits_of(size))]


def sum_gram(me, size, gram_ref, parts, arrived, send_sem, recv_sem):
    if not direct_sum(parts.shape[0] * parts.shape[1], size):
        gram_ref[...] = parts[...].reshape(gram_ref.shape)
        for stage in range(bits_of(size)):
            copy = remote(
                gram_ref,
                arrived.at[stage],
                send_sem.at[stage],
                recv_sem.at[stage],
                partner_of(me, 1 << stage),
            )
            copy.start()
            copy.wait()
            gram_ref[...] += arrived[stage]
        return
    height = parts.shape[1]
    scatter = [
        remote(
            parts.at[partner_of(me, d)],
            arrived.at[d],
            send_sem.at[d],
            recv_sem.at[d],
            partner_of(me, d),
        )
        for d in range(1, size)
    ]
    for copy in scatter:
        copy.start()
    total = parts[me]
    for d, copy in enumerate(scatter, 1):
        copy.wait_recv()
        total = total + arrived[d]
    arrived[0] = total
    own = pl.ds(pl.multiple_of(me * height, height), height)
    gather = [
        remote(
            arrived.at[0],
            gram_ref.at[own],
            send_sem.at[size + d],
            recv_sem.at[size + d],
            partner_of(me, d),
        )
        for d in range(1, size)
    ]
    for copy in gather:
        copy.start()
    gram_ref[own, :] = total
    for copy in gather:
        copy.wait_recv()
    for copy in scatter + gather:
        copy.wait_send()


def sketch_kernel(
    size,
    group_ref,
    live_ref,
    image_ref,
    matrix_ref,
    filters,
    pair_ref,
    pair_t_ref,
    table_ref,
    table_t_ref,
    out_ref,
    sketch_ref,
    gram_ref,
    turned,
    held,
    summed,
    parts,
    arrived,
    send_sem,
    recv_sem,
    sum_send_sem,
    sum_recv_sem,
):
    me = lax.axis_index("pix")
    step = pl.program_id(0)
    steps = out_ref.shape[1] // image_ref.shape[0]
    count, length, _ = image_ref.shape
    pairs = count // 2
    base = step * count
    orders = gathering_orders(size)
    stages = bits_of(size)
    height = matrix_ref.shape[0] // 2

    def copy_of(half, stage, mask):
        bit = orders[half][stage]
        slot = (bit | mask) - 1
        return remote(
            held.at[half, mask],
            held.at[half, bit | mask],
            send_sem.at[half, slot],
            recv_sem.at[half, slot],
            partner_of(me, bit),
        )

    def receive(stage, half, mask):
        copy_of(half, stage, mask).wait_recv()
        for later in range(stage + 1, stages):
            copy_of(half, later, orders[half][stage] | mask).start()

    @pl.when(step == 0)
    def _():
        greet(me, peers(gram_ref.shape[0], size))
        for half in range(2):
            held[half, 0] = matrix_ref[half * height : (half + 1) * height, :]
        for stage in range(stages):
            for half in range(2):
                copy_of(half, stage, 0).start()

    early = min(2, stages)
    for stage in range(early):

        @pl.when(step == steps * (5 + 6 * stage) // 16)
        def _(stage=stage):
            for place in range(1 << stage):
                for half in range(2):
                    receive(stage, half, sums(orders[half][:stage])[place])

    def side_by_side(values):
        return jnp.concatenate(values, axis=1)

    def stacked(wide):
        return jnp.concatenate(
            [wide[:, 2 * length * i : 2 * length * (i + 1)] for i in range(pairs)], axis=0
        )

    def unstacked(tall):
        return side_by_side([tall[length * i : length * (i + 1)] for i in range(pairs)])

    images = jnp.concatenate(
        [side_by_side([image_ref[2 * i], image_ref[2 * i + 1]]) for i in range(pairs)], axis=0
    )
    rows = jnp.dot(images, pair_ref[...], preferred_element_type=F32).astype(BF16)
    spectrum = jnp.dot(table_t_ref[...], unstacked(rows), preferred_element_type=F32)
    weights = side_by_side([filters[group_ref[base + i]] for i in range(count)])
    kept = (spectrum * weights.astype(F32)).astype(BF16)
    back = jnp.dot(stacked(kept), pair_t_ref[...], preferred_element_type=F32).astype(BF16)
    result = jnp.dot(table_ref[...], unstacked(back), preferred_element_type=F32)
    for i in range(count):
        turned[pl.ds(i, length, stride=count), :] = result[:, i * length : (i + 1) * length]
    slot = base + lax.broadcasted_iota(jnp.int32, (1, count, 1), 1)
    values = turned[...].reshape(length, count, length)
    out_ref[:, pl.ds(pl.multiple_of(base, count), count), :] = jnp.where(
        slot < live_ref[0], values, 0.0
    ).astype(BF16)

    @pl.when(step == steps - 1)
    def _():
        lines = length // size
        part = lines // 2

        def term(half, mask):
            start = partner_of(me, mask) * lines + half * part
            left = side_by_side([out_ref[start + line] for line in range(part)])
            return jnp.dot(left, held[half, mask], preferred_element_type=F32)

        sketch_ref[...] = jnp.zeros_like(sketch_ref)
        for half in range(2):
            for mask in sums(orders[half][:early]):
                sketch_ref[...] += term(half, mask)
        for stage in range(early, stages):
            for place in range(1 << stage):
                for half in range(2):
                    mask = sums(orders[half][:stage])[place]
                    receive(stage, half, mask)
                    sketch_ref[...] += term(half, orders[half][stage] | mask)
        sketch = sketch_ref[...]
        gram = lax.dot_general(
            sketch, sketch, (((0,), (0,)), ((), ())), precision=HIGHEST, preferred_element_type=F32
        )
        parts[...] = gram.reshape(parts.shape)
        sum_gram(me, size, summed, parts, arrived, sum_send_sem, sum_recv_sem)
        gram_ref[...] = summed[...]
        for half in range(2):
            for stage in range(stages):
                for mask in sums(orders[half][:stage]):
                    copy_of(half, stage, mask).wait_send()


def make_sketch(images, groups, live, defocus_values, matrix, size):
    slots, length, _ = images.shape
    height, rank = matrix.shape
    count = math.gcd(slots, 16)
    table = real_tables(length)
    zero = jnp.zeros_like(table)
    pair = jnp.concatenate(
        [jnp.concatenate([table, zero], axis=1), jnp.concatenate([zero, table], axis=1)], axis=0
    )
    number = defocus_values.shape[0]
    if direct_sum(rank, size):
        summing = [
            pltpu.VMEM((size, rank // size, rank), F32),
            pltpu.VMEM((size, rank // size, rank), F32),
        ]
        signals = 2 * size
    else:
        summing = [
            pltpu.VMEM((1, rank, rank), F32),
            pltpu.VMEM((bits_of(size), rank, rank), F32),
        ]
        signals = bits_of(size)

    def whole(*shape):
        return pl.BlockSpec(shape, lambda i, *_: (0,) * len(shape))

    return pl.pallas_call(
        functools.partial(sketch_kernel, size),
        out_shape=(
            jax.ShapeDtypeStruct((length, slots, length), BF16),
            jax.ShapeDtypeStruct((slots, rank), F32),
            jax.ShapeDtypeStruct((rank, rank), F32),
        ),
        grid_spec=pltpu.PrefetchScalarGridSpec(
            num_scalar_prefetch=2,
            grid=(slots // count,),
            in_specs=[
                pl.BlockSpec((count, length, length), lambda i, *_: (i, 0, 0)),
                whole(height, rank),
                whole(number, length, length),
                whole(2 * length, 2 * length),
                whole(2 * length, 2 * length),
                whole(length, length),
                whole(length, length),
            ],
            out_specs=(whole(length, slots, length), whole(slots, rank), whole(rank, rank)),
            scratch_shapes=[
                pltpu.VMEM((length * count, length), F32),
                pltpu.VMEM((2, size, height // 2, rank), BF16),
                pltpu.VMEM((rank, rank), F32),
                *summing,
                pltpu.SemaphoreType.DMA((2, size - 1)),
                pltpu.SemaphoreType.DMA((2, size - 1)),
                pltpu.SemaphoreType.DMA((signals,)),
                pltpu.SemaphoreType.DMA((signals,)),
            ],
        ),
        compiler_params=pltpu.CompilerParams(
            collective_id=0, has_side_effects=True, vmem_limit_bytes=50 << 20
        ),
        name="sketch",
    )(
        groups,
        live,
        images,
        matrix,
        filter_table(defocus_values, length),
        pair,
        pair.T,
        table,
        table.T,
    )


def basis_kernel(factor_ref, sketch_ref, out_ref, turned_ref):
    rank = factor_ref.shape[0]
    row = lax.broadcasted_iota(jnp.int32, (rank, rank), 0)
    col = lax.broadcasted_iota(jnp.int32, (rank, rank), 1)
    factor = factor_ref[...]
    on_diagonal = jnp.where(row == col, factor, 0.0)
    lower = jnp.where(row > col, factor, 0.0) / jnp.sum(on_diagonal, axis=1, keepdims=True)

    def times(left, right):
        return jnp.dot(left, right, precision=HIGHEST, preferred_element_type=F32)

    def same_block(shift):
        return lax.shift_right_logical(row, shift) == lax.shift_right_logical(col, shift)

    shift = 3
    within = jnp.where(same_block(shift), lower, 0.0)
    unit = jnp.where(row == col, 1.0, 0.0).astype(F32)
    square = times(within, within)
    fourth = times(square, square)
    inverse = times(times(unit - within, unit + square), unit + fourth)
    while 1 << shift < rank:
        off = jnp.where(same_block(shift + 1) & ~same_block(shift), lower, 0.0)
        inverse = inverse - times(inverse, times(off, inverse))
        shift += 1
    inverse = inverse / jnp.sum(on_diagonal, axis=0, keepdims=True)
    basis = lax.dot_general(
        sketch_ref[...],
        inverse,
        (((1,), (1,)), ((), ())),
        precision=HIGHEST,
        preferred_element_type=F32,
    )
    out_ref[...] = basis.astype(BF16)
    turned_ref[...] = basis.T.astype(BF16)


def make_basis(factor_low, sketch):
    slots, rank = sketch.shape
    return pl.pallas_call(
        basis_kernel,
        out_shape=(
            jax.ShapeDtypeStruct((slots, rank), BF16),
            jax.ShapeDtypeStruct((rank, slots), BF16),
        ),
        name="basis",
    )(factor_low, sketch)


def project_kernel(size, basis_ref, column_ref, out_ref, held, arrived, send_sem, recv_sem):
    me = lax.axis_index("pix")
    length = column_ref.shape[0]
    rows = length // size
    part = rows // 2
    orders = halving_orders(size)
    slots = {}
    for half in range(2):
        for stage in range(len(orders[half])):
            for mask in masks_of(orders[half][stage + 1 :]):
                slots[half, stage, mask] = len(slots) % (size - 1)

    def copy_of(half, stage, mask):
        bit = orders[half][stage]
        slot = slots[half, stage, mask]
        return remote(
            held.at[half, bit | mask],
            arrived.at[half, slot],
            send_sem.at[half, slot],
            recv_sem.at[half, slot],
            partner_of(me, bit),
        )

    greet(me, [1 << shift for shift in range(bits_of(size))])
    first = orders[0][0]

    def compute(half, mask):
        start = partner_of(me, mask) * rows + half * part
        right = jnp.concatenate([column_ref[start + row] for row in range(part)], axis=1)
        held[half, mask] = jnp.dot(
            basis_ref[...], right, preferred_element_type=F32
        ).astype(BF16)

    def add(half, stage, mask):
        later = orders[half][stage + 1 :]
        copy_of(half, stage, mask).wait_recv()
        total = (
            held[half, mask].astype(F32)
            + arrived[half, slots[half, stage, mask]].astype(F32)
        )
        if later:
            held[half, mask] = total.astype(BF16)
            if mask & later[0]:
                copy_of(half, stage + 1, mask - later[0]).start()
        else:
            height = out_ref.shape[0] // 2
            out_ref[half * height : (half + 1) * height, :] = total.T

    kept = [masks_of(orders[half][1:]) for half in range(2)]
    for place in range(len(kept[0]) + 1):
        for half in range(2):
            if place < len(kept[0]):
                mask = kept[half][place]
                compute(half, first | mask)
                copy_of(half, 0, mask).start()
                compute(half, mask)
        for half in range(2):
            if place > 0:
                add(half, 0, kept[half][place - 1])
    for stage in range(1, bits_of(size)):
        for place in range(len(masks_of(orders[0][stage + 1 :]))):
            for half in range(2):
                add(half, stage, masks_of(orders[half][stage + 1 :])[place])
    for half in range(2):
        for stage in range(bits_of(size)):
            for mask in masks_of(orders[half][stage + 1 :]):
                copy_of(half, stage, mask).wait_send()


def project(columns, basis_t, size):
    length, slots, _ = columns.shape
    rank = basis_t.shape[0]
    width = length * length // size
    return pl.pallas_call(
        functools.partial(project_kernel, size),
        out_shape=jax.ShapeDtypeStruct((width, rank), F32),
        in_specs=[pl.BlockSpec(memory_space=pltpu.VMEM)] * 2,
        out_specs=pl.BlockSpec(memory_space=pltpu.VMEM),
        scratch_shapes=[
            pltpu.VMEM((2, size, rank, width // 2), BF16),
            pltpu.VMEM((2, size - 1, rank, width // 2), BF16),
            pltpu.SemaphoreType.DMA((2, size - 1)),
            pltpu.SemaphoreType.DMA((2, size - 1)),
        ],
        compiler_params=pltpu.CompilerParams(
            collective_id=1, has_side_effects=True, vmem_limit_bytes=48 << 20
        ),
        name="project",
    )(basis_t, columns)


def per_device(particle_images, defocus_group, live_counts, defocus_values, test_matrix):
    size = lax.axis_size("pix")
    columns, sketch, gram = make_sketch(
        particle_images, defocus_group, live_counts, defocus_values, test_matrix, size
    )
    factor_low = jnp.linalg.cholesky(gram)
    range_basis, basis_t = make_basis(factor_low, sketch)
    return (range_basis, project(columns, basis_t, size))


def solution(mesh):
    placed = (
        P(("grp", "pix"), None, None),
        P(("grp", "pix")),
        P(("grp", "pix")),
        P("grp"),
        P(("grp", "pix"), None),
    )
    return jax.shard_map(
        per_device,
        mesh=mesh,
        in_specs=placed,
        out_specs=(P(("grp", "pix"), None), P(("grp", "pix"), None)),
        check_vma=False,
    )
```
